512 devices in a mesh: expert: 16 (over x, y_hi), tensor: 32 (over z, y_lo, core).
Axes of the slice: x: 4, y: 8 (y_hi: 4, y_lo: 2; y = y_hi * 2 + y_lo), z: 8, core: 2. Of those that a mesh axis runs over, the one named last changes fastest.
Arguments:
- tokens: bfloat16 [2048, 6144], P('expert'), may hold values from -6 to 6
- routes: int32 [2048, 4], P('expert'), may hold values from 0 to 15, all different within a row; in each aligned block of 128 rows (0 to 127, 128 to 255, ...) at most 40 rows name the same one
- gates: float32 [2048, 4], P('expert'), may hold values from 0.05 to 1
- gate_proj: bfloat16 [16, 2688, 6144], P('expert', 'tensor'), may hold values from -0.078125 to 0.078125
- up_proj: bfloat16 [16, 2688, 6144], P('expert', 'tensor'), may hold values from -0.078125 to 0.078125
- down_proj: bfloat16 [16, 6144, 2688], P('expert', 'tensor'), may hold values from -0.0625 to 0.0625
Outputs:
- combined: bfloat16 [2048, 6144], P('expert', 'tensor')
The draws below stay inside these ranges and needn't reach their ends.
Inputs may be any that keep to these rules, and one draw needn't show every extreme that they name: `routes`: the ids of one row are distinct. In each aligned block of 128 rows no id is named by more than 40 rows, a bound that some block reaches.
All inputs are finite; a program needn't handle non-finite values.
Results may differ from the reference program's by a relative error of at most 0.0057.
Values may be sent and summed in bfloat16 or wider, within the bound.
No kernel may reach another device: no remote copies, remote signals or barrier semaphores. Data moves between devices by JAX's collectives and lax.ppermute only.
A program may use at most 64 MiB of HBM per device.

```python
import math
import jax
import jax.numpy as jnp
import numpy as np
from jax import lax

D = 6144
FF = 10752
EXPERTS = 16
TOP = 4
WIN = 4
ROWS_DEV = 128
CAP = 40
FF_G = 2688
GROUPS = 16
ROWS = 2048


def steps_of(key, dims, cuts, low, largest):
    gain, own = 1.0, jax.random.fold_in(key, 6)
    for dim, blocks in cuts:
        steps = jnp.exp(jax.random.uniform(jax.random.fold_in(own, dim), (blocks,), jnp.float32, low / len(cuts), largest / len(cuts)))
        gain = gain * jnp.repeat(steps, dims[dim] // blocks).reshape([-1 if axis == dim else 1 for axis in range(len(dims))])
    return gain


def shared_out(own_key, own, number, rows, count, top, most, slope):
    sequence = jax.random.permutation(own_key, count)
    crowded, common = shares(count, rows * top, most, slope, True), shares(count, rows * top, most, slope, False)
    places = jnp.arange(count)

    def named(lengths, rotation):
        used = int((lengths > 0).sum())
        fixed = max(1, used // 4)
        shifted = fixed + (places - fixed + rotation * (used - fixed)) % max(1, count - fixed)
        return jnp.zeros((count,), jnp.int32).at[sequence[jnp.where(places < fixed, places, shifted)]].set(jnp.asarray(lengths, jnp.int32))

    lengths = jnp.where(number % 4 == 0, named(crowded, number // 4), named(common, number - number // 4 - 1))
    mixed = jax.random.permutation(jax.random.fold_in(own, 3), count)
    giver, receiver = mixed[0:count // 2 * 2:2], mixed[1:count // 2 * 2:2]
    slack = jnp.minimum(lengths[giver] - 1, most - lengths[receiver]) // 2
    slack = jnp.where((giver == sequence[0]) | (receiver == sequence[0]) | (lengths[receiver] == 0), 0, jnp.maximum(slack, 0))
    shifted = jax.random.randint(jax.random.fold_in(own, 4), (count // 2,), 0, 1 << 20) % (slack + 1)
    lengths = lengths.at[giver].add(-shifted).at[receiver].add(shifted)
    labels = jnp.searchsorted(jnp.cumsum(lengths), jnp.arange(rows * top), side="right").astype(jnp.int32)
    table = labels.reshape(top, rows).T
    table = table[jax.random.permutation(jax.random.fold_in(own, 1), rows)]
    rotation = jax.random.randint(jax.random.fold_in(own, 2), (rows, 1), 0, top)
    return jnp.take_along_axis(table, (jnp.arange(top)[None, :] + rotation) % top, axis=1)


def shares(count, total, bound, lean, full):
    portions = [(1 << 20) // math.isqrt(grade ** lean) + 1 for grade in range(1, count + 1)]
    largest = bound if full else min(bound, max(-(-total // count), total * portions[0] // sum(portions)))
    least = 1 if total - largest >= count - 1 else 0
    given, spare = [largest] + [least] * (count - 1), total - largest - least * (count - 1)
    while spare > 0:
        movable = [i for i in range(1, count) if given[i] < largest] or [i for i in range(1, count) if given[i] < bound]
        pool, budget = sum([portions[i] for i in movable]), spare
        for i in movable:
            addition = min(bound - given[i], max(1, budget * portions[i] // pool), spare)
            given[i] = given[i] + addition
            spare = spare - addition
    return np.array(given)


def bell_draw(rng, dims, spread, bound, pieces=(), kind=jnp.bfloat16):
    entries = spread * jax.random.normal(rng, dims, jnp.float32)
    if pieces:
        entries = entries * steps_of(rng, dims, pieces, -0.22, 0.18)
    return jnp.clip(entries, -bound, bound).astype(kind)


def setup_inputs(seed: int = 0) -> dict:
    streams_of = jax.random.split(jax.random.key(seed), 7)
    tokens = bell_draw(streams_of[0], (ROWS, D), 1.0, 6.0, ((0, 16),))
    routes_keys = jax.random.split(jax.random.fold_in(streams_of[1], 1), ROWS // ROWS_DEV)
    routes_turns = jax.random.permutation(jax.random.fold_in(streams_of[1], 3), ROWS // ROWS_DEV)
    routes = jax.vmap(lambda own, number: shared_out(jax.random.fold_in(streams_of[1], 2), own, number, ROWS_DEV, EXPERTS, TOP, CAP, 2))(routes_keys, routes_turns).reshape((ROWS, TOP))
    gates = jnp.clip(jnp.exp(math.log(1.0) - 2.9957323 * jax.random.uniform(streams_of[2], (ROWS, TOP), jnp.float32) ** steps_of(streams_of[2], (ROWS, TOP), ((0, 16),), -0.2, 0.2)), 0.05, 1.0)
    gate_proj = bell_draw(streams_of[3], (GROUPS, FF_G, D), D ** -0.5, 0.078125, ((0, 16), (1, 32)))
    up_proj = bell_draw(streams_of[4], (GROUPS, FF_G, D), D ** -0.5, 0.078125, ((0, 16), (1, 32)))
    down_proj = bell_draw(streams_of[5], (GROUPS, D, FF_G), FF ** -0.5, 0.0625, ((0, 16), (1, 32)))
    return {"tokens": tokens, "routes": routes, "gates": gates, "gate_proj": gate_proj, "up_proj": up_proj, "down_proj": down_proj}


def slot_tables(route_block, gate_block):
    row_count = route_block.shape[0]
    experts = jnp.arange(WIN, dtype=jnp.int32)
    hits = route_block[None, :, :] == experts[:, None, None]
    chosen = jnp.any(hits, axis=2)
    position = (jnp.cumsum(chosen.astype(jnp.int32), axis=1) - 1).astype(jnp.int32)
    slots = jnp.arange(CAP, dtype=jnp.int32)
    match = chosen[:, None, :] & (position[:, None, :] == slots[None, :, None])
    row_ids = jnp.arange(row_count, dtype=jnp.int32)
    row_index = jnp.sum(jnp.where(match, row_ids[None, None, :], 0), axis=2).astype(jnp.int32)
    filled = jnp.any(match, axis=2)
    weight = jnp.sum(jnp.where(hits, gate_block[None, :, :], jnp.zeros((), gate_block.dtype)), axis=2)
    return position, row_index, filled, weight


def reference(tokens, routes, gates, gate_proj, up_proj, down_proj):
    groups = gate_proj.shape[0]
    split = groups // WIN
    token_blocks = tokens.reshape(groups, ROWS_DEV, D)
    route_blocks = routes.reshape(groups, ROWS_DEV, TOP)
    gate_blocks = gates.reshape(groups, ROWS_DEV, TOP)
    position, row_index, filled, weight = jax.vmap(slot_tables)(route_blocks, gate_blocks)
    picked = jax.vmap(lambda block, index: jnp.take(block, index, axis=0))(token_blocks, row_index)
    picked = jnp.where(filled[..., None], picked, jnp.zeros((), tokens.dtype))
    per_expert = jnp.transpose(picked, (1, 0, 2, 3)).reshape(WIN, groups * CAP, D)

    def expert_group(group):
        dispatched = per_expert[group // split]
        gate_act = jnp.dot(dispatched, gate_proj[group].T, preferred_element_type=jnp.float32)
        up_act = jnp.dot(dispatched, up_proj[group].T, preferred_element_type=jnp.float32)
        hidden = (jax.nn.silu(gate_act) * up_act).astype(jnp.bfloat16)
        return jnp.dot(hidden, down_proj[group].T, preferred_element_type=jnp.float32).astype(jnp.bfloat16)

    partial_value = lax.map(expert_group, jnp.arange(groups, dtype=jnp.int32))
    expert_out = partial_value.astype(jnp.float32).reshape(WIN, split, groups, CAP, D).sum(axis=1)
    expert_out = jnp.transpose(expert_out, (1, 0, 2, 3))

    def combine(block_sum, block_position, block_weight):
        flat_sum = block_sum.reshape(WIN * CAP, D)
        offsets = jnp.arange(WIN, dtype=jnp.int32)[:, None] * CAP
        index = (offsets + jnp.clip(block_position, 0, CAP - 1)).astype(jnp.int32)
        values = jnp.take(flat_sum, index, axis=0)
        return jnp.sum(values * block_weight[..., None], axis=0)

    combined = jax.vmap(combine)(expert_out, position, weight)
    return combined.reshape(ROWS, D).astype(jnp.bfloat16)
```

```python
import jax
import jax.numpy as jnp
from jax import lax
from jax.sharding import Mesh, PartitionSpec as P

WIN = 4
CAP = 40
EXPERT = ("x", "yh")
TENSOR = ("zh", "zl", "yl", "c")
GROUP = ("zl", "yl", "c")
SIZES = (4, 4, 4, 2, 2, 2)


def slot_tables(route_block, gate_block):
    experts = jnp.arange(WIN, dtype=jnp.int32)
    hits = route_block[None, :, :] == experts[:, None, None]
    chosen = jnp.any(hits, axis=2)
    position = jnp.cumsum(chosen.astype(jnp.int32), axis=1) - 1
    slots = jnp.arange(CAP, dtype=jnp.int32)
    match = chosen[:, None, :] & (position[:, None, :] == slots[None, :, None])
    weight = jnp.sum(
        jnp.where(hits, gate_block[None, :, :], jnp.zeros((), gate_block.dtype)), axis=2
    )
    return match, weight


def contract_last(left, right):
    return lax.dot_general(
        left, right, (((1,), (1,)), ((), ())), preferred_element_type=jnp.float32
    )


def return_pairs():
    pairs = []
    for x in range(4):
        for yh in range(4):
            for q in range(8):
                turn = x * 4 + yh
                to_yh = q >> 1
                to_x = (q & 1) * 2 + (turn >> 3)
                to_q = turn & 7
                pairs.append(((x * 4 + yh) * 8 + q, (to_x * 4 + to_yh) * 8 + to_q))
    return pairs


def body(tokens, routes, gates, gate_proj, up_proj, down_proj):
    width = tokens.shape[1]
    part = width // 8
    hid = gate_proj.shape[1]
    out_w = down_proj.shape[1]
    q = lax.axis_index(GROUP)

    both = jnp.concatenate([gate_proj, up_proj], axis=0)
    both = both.reshape(2 * hid, 8, part).transpose(1, 0, 2)
    both = lax.all_to_all(both, GROUP, split_axis=0, concat_axis=0, tiled=True)
    w_gate = both[:, :hid].reshape(8 * hid, part)
    w_up = both[:, hid:].reshape(8 * hid, part)
    w_down = lax.all_gather(down_proj[0], GROUP, axis=0, tiled=True)

    match, weight = slot_tables(routes, gates)
    pick = match.reshape(WIN * CAP, -1)
    mine = lax.dynamic_slice_in_dim(tokens, q * part, part, axis=1)
    picked = jnp.dot(
        pick.astype(jnp.bfloat16), mine, preferred_element_type=jnp.float32
    ).astype(jnp.bfloat16)
    outgoing = jnp.broadcast_to(
        picked.reshape(1, WIN, CAP, part), (4, WIN, CAP, part)
    ).reshape(16, CAP, part)
    arrived = lax.all_to_all(outgoing, ("yh", "x"), split_axis=0, concat_axis=0, tiled=True)
    rows = arrived.reshape(16 * CAP, part)

    gate_part = contract_last(rows, w_gate).astype(jnp.bfloat16)
    up_part = contract_last(rows, w_up).astype(jnp.bfloat16)
    parts = jnp.concatenate([gate_part, up_part], axis=1).reshape(8, 2 * CAP, 16 * hid)
    parts = lax.all_to_all(parts, GROUP, split_axis=0, concat_axis=0, tiled=True)
    acts = jnp.sum(parts.astype(jnp.float32), axis=0)
    hidden = (jax.nn.silu(acts[:, : 8 * hid]) * acts[:, 8 * hid :]).astype(jnp.bfloat16)

    spread = jnp.broadcast_to(hidden[None], (4,) + hidden.shape)
    spread = lax.all_to_all(spread, "zh", split_axis=0, concat_axis=0, tiled=True)
    full = spread.transpose(1, 0, 2).reshape(2 * CAP, 32 * hid)
    partial_value = contract_last(full, w_down).astype(jnp.bfloat16)

    back = partial_value.reshape(2, CAP, 8, out_w).transpose(0, 2, 1, 3)
    back = back.reshape(16, CAP, out_w)
    back = lax.all_to_all(back, EXPERT, split_axis=0, concat_axis=0, tiled=True)
    summed = back.astype(jnp.float32).reshape(WIN, 4, CAP, out_w).sum(axis=1)
    summed = lax.ppermute(summed.reshape(WIN * CAP, out_w), EXPERT + GROUP, return_pairs())

    mix = jnp.where(match, weight[:, None, :], 0.0).reshape(WIN * CAP, -1)
    combined = lax.dot_general(
        mix,
        summed,
        (((0,), (0,)), ((), ())),
        precision=lax.Precision.HIGHEST,
        preferred_element_type=jnp.float32,
    )
    return combined.astype(jnp.bfloat16)


def solution(mesh):
    fine = Mesh(mesh.devices.reshape(SIZES), EXPERT + TENSOR)
    in_specs = (
        P(EXPERT, None),
        P(EXPERT, None),
        P(EXPERT, None),
        P(EXPERT, TENSOR, None),
        P(EXPERT, TENSOR, None),
        P(EXPERT, TENSOR, None),
    )
    return jax.shard_map(
        body, mesh=fine, in_specs=in_specs, out_specs=P(EXPERT, TENSOR), check_vma=False
    )
```

```python
import jax
import jax.numpy as jnp
from jax import lax
from jax.experimental import pallas as pl
from jax.experimental.pallas import tpu as pltpu
from jax.sharding import Mesh, PartitionSpec as P

WIN = 4
CAP = 40
EXPERT = ("x", "yh")
TENSOR = ("zh", "zl", "yl", "c")
GROUP = ("zl", "c")
SIZES = (4, 4, 4, 2, 2, 2)
VMEM = pl.BlockSpec(memory_space=pltpu.VMEM)
SMEM = pl.BlockSpec(memory_space=pltpu.SMEM)
ANY = pl.BlockSpec(memory_space=pl.ANY)


def slot_tables(route_block, gate_block):
    experts = jnp.arange(WIN, dtype=jnp.int32)
    hits = route_block[None, :, :] == experts[:, None, None]
    chosen = jnp.any(hits, axis=2)
    position = jnp.cumsum(chosen.astype(jnp.int32), axis=1) - 1
    slots = jnp.arange(CAP, dtype=jnp.int32)
    match = chosen[:, None, :] & (position[:, None, :] == slots[None, :, None])
    weight = jnp.sum(
        jnp.where(hits, gate_block[None, :, :], jnp.zeros((), gate_block.dtype)), axis=2
    )
    return match, weight


def contract_last(left, right):
    return lax.dot_general(
        left, right, (((1,), (1,)), ((), ())), preferred_element_type=jnp.float32
    )


def swap(value, mask):
    return lax.ppermute(value, GROUP, [(i, i ^ mask) for i in range(4)])


def ring_half(i):
    return i >> 1


def expert_groups():
    return [
        [(x * 4 + yh) * 2 + (g ^ ring_half(yh)) for yh in range(4) for x in range(4)]
        for g in range(2)
    ]


def depth_groups():
    return [
        [(zh * 2 + (g ^ ring_half(zh))) * 2 + yl for zh in range(4) for yl in range(2)]
        for g in range(2)
    ]


def return_pairs():
    pairs = []
    for x in range(4):
        for yh in range(4):
            for zh in range(4):
                for zl in range(2):
                    for yl in range(2):
                        for c in range(2):
                            chunk = (zl ^ ring_half(zh)) * 2 + c
                            to_zl, to_c = yh >> 1, yh & 1
                            pairs.append(
                                (
                                    ((((x * 4 + yh) * 4 + zh) * 2 + zl) * 2 + yl) * 2 + c,
                                    ((((x * 4 + chunk) * 4 + zh) * 2 + to_zl) * 2 + yl) * 2
                                    + to_c,
                                )
                            )
    return pairs


def pieces_kernel(q_ref, g0, u0, g1, u1, o0, o1):
    hid = g0.shape[1]
    for g_ref, u_ref, o_ref in ((g0, u0, o0), (g1, u1, o1)):
        o_ref[0, :hid] = g_ref[0]
        o_ref[0, hid:] = u_ref[0]


def weight_pieces(q, gate_proj, up_proj):
    hid, width = gate_proj.shape[1:]
    part = width // 4

    def source(m):
        return pl.BlockSpec((1, hid, part), lambda r, q_ref: (0, 0, q_ref[0] ^ (2 * m + r)))

    return pl.pallas_call(
        pieces_kernel,
        out_shape=[jax.ShapeDtypeStruct((2, 2 * hid, part), gate_proj.dtype)] * 2,
        grid_spec=pltpu.PrefetchScalarGridSpec(
            num_scalar_prefetch=1,
            grid=(2,),
            in_specs=[source(0), source(0), source(1), source(1)],
            out_specs=[pl.BlockSpec((1, 2 * hid, part), lambda r, q_ref: (r, 0, 0))] * 2,
        ),
        cost_estimate=pl.CostEstimate(flops=0, bytes_accessed=8 << 20, transcendentals=0),
        name="weight_pieces",
    )(q, gate_proj, up_proj, gate_proj, up_proj)


def pack_kernel(q_ref, r0, r1, c_ref, out_ref, sems):
    q = q_ref[0]
    copies = []
    for m, r_ref in enumerate((r0, r1)):
        copies.append((r_ref.at[0], out_ref.at[(2 * m) ^ q]))
        copies.append((c_ref.at[m], out_ref.at[(2 * m + 1) ^ q]))
    copies = [
        pltpu.make_async_copy(source, target, sems.at[i])
        for i, (source, target) in enumerate(copies)
    ]
    for copy in copies:
        copy.start()
    for copy in copies:
        copy.wait()


def pack_weights(q, direct, crossed):
    both, part = crossed.shape[1:]
    packed = pl.pallas_call(
        pack_kernel,
        out_shape=jax.ShapeDtypeStruct((4, both, part), crossed.dtype),
        in_specs=[SMEM] + [ANY] * 3,
        out_specs=ANY,
        scratch_shapes=[pltpu.SemaphoreType.DMA((4,))],
        compiler_params=pltpu.CompilerParams(vmem_limit_bytes=1 << 20),
        cost_estimate=pl.CostEstimate(flops=0, bytes_accessed=4 << 20, transcendentals=0),
        name="pack_weights",
    )(q, *direct, crossed)
    return packed.reshape(4 * both, part)


def first_kernel(q_ref, x_ref, packed, other_ref, own_ref):
    core = lax.rem(q_ref[0], 2)
    flip = q_ref[1]
    width = packed.shape[0]
    rows = 4 * CAP
    for side, out_ref in ((1 - core, other_ref), (core, own_ref)):
        for m in range(2):
            start = pl.multiple_of(((2 * m) ^ flip) * rows + side * rows, 16)
            value = x_ref[pl.ds(start, rows)]
            for n in range(0, width, 256):
                stop = min(n + 256, width)
                out_ref[m, :, n:stop] = contract_last(value, packed[n:stop])


def first_matmul(q, rows, packed):
    width, part = packed.shape
    shape = jax.ShapeDtypeStruct((2, 4 * CAP, width), jnp.float32)
    return pl.pallas_call(
        first_kernel,
        out_shape=[shape, shape],
        in_specs=[SMEM, VMEM, VMEM],
        out_specs=[VMEM, VMEM],
        compiler_params=pltpu.CompilerParams(vmem_limit_bytes=24 << 20),
        cost_estimate=pl.CostEstimate(
            flops=2 * 640 * 672 * 1536, bytes_accessed=7 << 20, transcendentals=0
        ),
        name="first_matmul",
    )(q, rows, packed)


def activations_kernel(own_ref, near_ref, far_ref, out_ref):
    acts = own_ref[...] + near_ref[...] + far_ref[...].astype(jnp.float32)
    hid = acts.shape[1] // 8
    for j in range(4):
        gate = acts[:, 2 * hid * j : 2 * hid * j + hid]
        up = acts[:, 2 * hid * j + hid : 2 * hid * (j + 1)]
        hidden = ((gate / (1.0 + jnp.exp(-gate))) * up).astype(jnp.bfloat16)
        for z in range(8):
            out_ref[z, :, hid * j : hid * (j + 1)] = hidden


def activations(own, near, far):
    rows, width = own.shape
    return pl.pallas_call(
        activations_kernel,
        out_shape=jax.ShapeDtypeStruct((8, rows, width // 2), jnp.bfloat16),
        in_specs=[VMEM] * 3,
        out_specs=VMEM,
        compiler_params=pltpu.CompilerParams(vmem_limit_bytes=20 << 20),
        cost_estimate=pl.CostEstimate(
            flops=1 << 20, bytes_accessed=3 << 20, transcendentals=1 << 16
        ),
        name="activations",
    )(own, near, far)


def second_kernel(q_ref, h_ref, d0, d1, d2, d3, out_ref, full):
    q = q_ref[0]
    part = h_ref.shape[2] // 2
    for zh in range(4):
        for zl in range(2):
            for yl in range(2):
                start = ((zh * 2 + zl) * 2 + yl) * part
                full[:, start : start + part] = h_ref[
                    zh * 2 + yl, :, zl * part : (zl + 1) * part
                ]
    value = full[...]
    for k, d_ref in enumerate((d0, d1, d2, d3)):
        out_ref[k ^ q] = contract_last(value, d_ref[...]).astype(jnp.bfloat16)


def second_matmul(q, spread, downs):
    rows = spread.shape[1]
    out_w, depth = downs[0].shape
    return pl.pallas_call(
        second_kernel,
        out_shape=jax.ShapeDtypeStruct((4, rows, out_w), jnp.bfloat16),
        in_specs=[SMEM] + [VMEM] * 5,
        out_specs=VMEM,
        scratch_shapes=[pltpu.VMEM((rows, depth), jnp.bfloat16)],
        compiler_params=pltpu.CompilerParams(vmem_limit_bytes=24 << 20),
        cost_estimate=pl.CostEstimate(
            flops=2 * 160 * 768 * 2688, bytes_accessed=6 << 20, transcendentals=0
        ),
        name="second_matmul",
    )(q, spread, *downs)


def body(tokens, routes, gates, gate_proj, up_proj, down_proj):
    width = tokens.shape[1]
    part = width // 4
    out_w = down_proj.shape[1]
    q = lax.axis_index(GROUP)
    q1 = q.reshape(1)
    zl = lax.axis_index("zl")
    flip = 2 * ring_half(lax.axis_index("zh"))
    down0 = down_proj[0]

    p0, p1 = weight_pieces(q1, gate_proj, up_proj)
    direct = (p0, swap(p1, 2))
    crossed = swap(jnp.stack([d[1] for d in direct]), 1)
    packed = pack_weights(q1, direct, crossed)

    match, weight = slot_tables(routes, gates)
    pick = match.reshape(WIN * CAP, -1)
    mine = lax.dynamic_slice_in_dim(tokens, q * part, part, axis=1)
    picked = jnp.dot(
        pick.astype(jnp.bfloat16), mine, preferred_element_type=jnp.float32
    ).astype(jnp.bfloat16)
    outgoing = jnp.broadcast_to(
        picked.reshape(1, WIN, CAP, part), (4, WIN, CAP, part)
    ).reshape(16, CAP, part)
    arrived = lax.all_to_all(
        outgoing,
        ("x", "yh", "yl"),
        split_axis=0,
        concat_axis=0,
        axis_index_groups=expert_groups(),
        tiled=True,
    )
    late, crossed_now = lax.optimization_barrier((down0, crossed))
    down_z = swap(late, 2)
    cross_0 = swap(late, 1)
    cross_z = swap(down_z, 1)
    arrived, down_z, cross_0, cross_z = lax.optimization_barrier(
        (arrived, down_z, cross_0, cross_z)
    )
    rows = arrived.reshape(16 * CAP, part)

    other, own = first_matmul(jnp.stack([q, flip]), rows, packed)
    near = swap(other, 1)
    mine_own = lax.dynamic_index_in_dim(own, zl, axis=0, keepdims=False)
    mine_near = lax.dynamic_index_in_dim(near, zl, axis=0, keepdims=False)
    theirs = lax.dynamic_index_in_dim(own, 1 - zl, axis=0, keepdims=False)
    theirs += lax.dynamic_index_in_dim(near, 1 - zl, axis=0, keepdims=False)
    far = swap(theirs.astype(jnp.bfloat16), 2)
    spread = activations(mine_own, mine_near, far)

    spread = lax.all_to_all(
        spread,
        ("zh", "zl", "yl"),
        split_axis=0,
        concat_axis=0,
        axis_index_groups=depth_groups(),
        tiled=True,
    )
    back = second_matmul(q1, spread, (down0, cross_0, down_z, cross_z))
    back = back.reshape(16, CAP, out_w)
    back = lax.all_to_all(back, ("yh", "x"), split_axis=0, concat_axis=0, tiled=True)
    summed = back.astype(jnp.float32).reshape(4, WIN, CAP, out_w).sum(axis=0)
    summed = summed.astype(jnp.bfloat16).reshape(WIN * CAP, out_w)
    summed = lax.ppermute(summed, EXPERT + TENSOR, return_pairs())

    mix = jnp.where(match, weight[:, None, :], 0.0).reshape(WIN * CAP, -1)
    combined = lax.dot_general(
        mix,
        summed.astype(jnp.float32),
        (((0,), (0,)), ((), ())),
        precision=lax.Precision.HIGHEST,
        preferred_element_type=jnp.float32,
    )
    return combined.astype(jnp.bfloat16)


def solution(mesh):
    fine = Mesh(mesh.devices.reshape(SIZES), EXPERT + TENSOR)
    in_specs = (
        P(EXPERT, None),
        P(EXPERT, None),
        P(EXPERT, None),
        P(EXPERT, TENSOR, None),
        P(EXPERT, TENSOR, None),
        P(EXPERT, TENSOR, None),
    )
    return jax.shard_map(
        body, mesh=fine, in_specs=in_specs, out_specs=P(EXPERT, TENSOR), check_vma=False
    )
```
